32 devices in a mesh: section: 8 (over z, core), tensor: 2 (over x), replica: 2 (over y).
Axes of the slice: x: 2, y: 2, z: 4, core: 2. Of those that a mesh axis runs over, the one named last changes fastest.
Arguments:
- pool_inputs: bfloat16 [8, 256, 2, 1408], P('section', 'replica', None, 'tensor'), may hold values from -6 to 6
- pool_mixed: bfloat16 [8, 256, 1408], P('section', 'replica'), may hold values from -6 to 6
- crop_ids: int32 [8, 8, 128], P('section', 'replica'), may hold values from 0 to 127
- incoming: bfloat16 [8, 256, 1408], P('section', 'replica', 'tensor'), may hold values from -6 to 6
- loss_grads: bfloat16 [3, 256, 1408], P(None, 'replica', 'tensor'), may hold values from -6 to 6
- w_proj: bfloat16 [8, 2, 1408, 1408], P('section', None, ('tensor', 'replica')), may hold values from -0.109375 to 0.109375
- w_up: bfloat16 [8, 1408, 3072], P('section', None, ('tensor', 'replica')), may hold values from -0.15625 to 0.15625
- w_down: bfloat16 [8, 3072, 1408], P('section', ('tensor', 'replica')), may hold values from -0.109375 to 0.109375
Outputs:
- grad_proj: bfloat16 [8, 2, 1408, 1408], P('section', None, ('tensor', 'replica'))
- grad_up: bfloat16 [8, 1408, 3072], P('section', None, ('tensor', 'replica'))
- grad_down: bfloat16 [8, 3072, 1408], P('section', ('tensor', 'replica'))
- outgoing: bfloat16 [8, 256, 2, 1408], P('section', 'replica', None, 'tensor')
The draws below stay inside these ranges and needn't reach their ends.
All inputs are finite; a program needn't handle non-finite values.
Results may differ from the reference program's by a relative error of at most 0.02.
Values may be sent and summed in bfloat16 or wider, within the bound.
A program may use at most 128 MiB of HBM per device.

```python
import math
import jax
import jax.numpy as jnp
import numpy as np
from jax import lax

D = 1408
FF = 3072
M = 128
TICKS = 4
POOL = 128
SECTIONS = 8
REPLICAS = 2


def set_ends(drawn, stream_key, low, high):
    longest = drawn.shape.index(max(drawn.shape))
    spots = []
    for shift in (0, 1):
        where = [jax.random.randint(jax.random.fold_in(stream_key, axis), (), 0, length) for axis, length in enumerate(drawn.shape)]
        where[longest] = (where[longest] + shift) % drawn.shape[longest]
        spots.append(tuple(where))
    return drawn.at[spots[0]].set(low).at[spots[1]].set(high)


def shard_levels(stream_key, dims, cuts, smallest, top_value):
    factor_of, own = 1.0, jax.random.fold_in(stream_key, 6)
    for position, shards_of in cuts:
        draws = jnp.exp(jax.random.uniform(jax.random.fold_in(own, position), (shards_of,), jnp.float32, smallest / len(cuts), top_value / len(cuts)))
        factor_of = factor_of * jnp.repeat(draws, dims[position] // shards_of).reshape([-1 if axis == position else 1 for axis in range(len(dims))])
    return factor_of


def rank_bounds(count, lean):
    loads = [(1 << 20) // math.isqrt(rank ** lean) + 1 for rank in range(1, count + 1)]
    width = 1 + sum(loads) // (1 << 30)
    return np.cumsum(np.array([max(1, weight // width) for weight in loads]))


def ranked(key, shape, number_of, slope):
    listing = rank_bounds(number_of, slope)
    lot = jax.random.randint(jax.random.fold_in(key, 1), shape, 0, int(listing[number_of - 1]))
    rank = jnp.searchsorted(jnp.asarray(listing, jnp.int32), lot, side="right")
    return jax.random.permutation(jax.random.fold_in(key, 2), number_of)[rank].astype(jnp.int32)


def noise(rng, extent, width, limit, split=(), kind=jnp.bfloat16):
    factor_of = shard_levels(rng, extent, split, -0.22, 0.18) if split else 1.0
    array = jax.random.normal(rng, extent, jnp.float32) * width * factor_of
    return jnp.minimum(jnp.maximum(array, -limit), limit).astype(kind)


def setup_inputs(seed: int = 0) -> dict:
    key_of = jax.random.split(jax.random.key(seed), 9)
    return {
        "pool_inputs": noise(key_of[0], (SECTIONS, REPLICAS * POOL, 2, D), 1.0, 6.0, ((0, 8), (1, 2), (3, 2))),
        "pool_mixed": noise(key_of[1], (SECTIONS, REPLICAS * POOL, D), 1.0, 6.0, ((0, 8), (1, 2))),
        "crop_ids": set_ends(ranked(key_of[2], (SECTIONS, REPLICAS * TICKS, M), POOL, 2), jax.random.fold_in(key_of[2], 3), 0, POOL - 1).astype(jnp.int32),
        "incoming": noise(key_of[3], (SECTIONS, REPLICAS * M, D), 1.0, 6.0, ((0, 8), (1, 2), (2, 2))),
        "loss_grads": noise(key_of[4], (TICKS - 1, REPLICAS * M, D), 1.0, 6.0, ((1, 2), (2, 2))),
        "w_proj": noise(key_of[5], (SECTIONS, 2, D, D), (2 * D) ** -0.5, 0.109375, ((0, 8), (2, 4))),
        "w_up": noise(key_of[6], (SECTIONS, D, FF), D ** -0.5, 0.15625, ((0, 8), (2, 4))),
        "w_down": noise(key_of[7], (SECTIONS, FF, D), FF ** -0.5, 0.109375, ((0, 8), (1, 4))),
    }


gelu_scale = 0.7978845608
gelu_cubic = 0.044715


def gelu_pair(pre_gelu):
    inner = gelu_scale * (pre_gelu + gelu_cubic * pre_gelu * pre_gelu * pre_gelu)
    tanh_part = jnp.tanh(inner)
    gelu_value = 0.5 * pre_gelu * (1.0 + tanh_part)
    gelu_slope = 0.5 * (1.0 + tanh_part) + 0.5 * pre_gelu * (1.0 - tanh_part * tanh_part) * gelu_scale * (1.0 + 3.0 * gelu_cubic * pre_gelu * pre_gelu)
    return gelu_value, gelu_slope


def section_back(proj_weight, up_weight, down_weight, inputs, mixed_rows, upstream):
    pre_gelu = jnp.dot(mixed_rows, up_weight, preferred_element_type=jnp.float32)
    gelu_value, gelu_slope = gelu_pair(pre_gelu)
    activated = gelu_value.astype(jnp.bfloat16)
    back_act = jnp.dot(upstream, down_weight.T, preferred_element_type=jnp.float32)
    back_hidden = (back_act * gelu_slope).astype(jnp.bfloat16)
    back_mixed = upstream.astype(jnp.float32) + jnp.dot(back_hidden, up_weight.T, preferred_element_type=jnp.float32)
    mixed_grad = back_mixed.astype(jnp.bfloat16)
    input_grad = jnp.einsum('mj,kij->mki', mixed_grad.astype(jnp.float32), proj_weight.astype(jnp.float32)).astype(jnp.bfloat16)
    return activated, back_hidden, mixed_grad, input_grad


def finish(total):
    rounded = lax.optimization_barrier(total.astype(jnp.bfloat16))
    return jnp.sum(rounded.astype(jnp.float32), axis=0).astype(jnp.bfloat16)


def reference(pool_inputs, pool_mixed, crop_ids, incoming, loss_grads, w_proj, w_up, w_down):
    section_ids = jnp.arange(SECTIONS, dtype=jnp.int32)
    decoder_flag = (section_ids >= SECTIONS // 2).astype(jnp.float32)
    skip_mask = jnp.stack([jnp.ones((SECTIONS,), jnp.float32), decoder_flag], axis=1).astype(jnp.bfloat16)[:, None, :, None]
    encoder_weight = (section_ids < SECTIONS // 2).astype(jnp.float32)[:, None, None]
    offsets = (jnp.arange(REPLICAS, dtype=jnp.int32) * POOL)[None, :, None, None]
    row_ids = crop_ids.reshape(SECTIONS, REPLICAS, TICKS, M).astype(jnp.int32) + offsets
    upstream = incoming
    seen_inputs, seen_mixed, seen_upstream = [], [], []
    input_grad = None
    for tick_index in range(TICKS):
        picked_rows = row_ids[:, :, tick_index, :].reshape(SECTIONS, REPLICAS * M)
        inputs = jax.vmap(lambda source_rows, chosen: source_rows[chosen])(pool_inputs, picked_rows) * skip_mask
        mixed_rows = jax.vmap(lambda source_rows, chosen: source_rows[chosen])(pool_mixed, picked_rows)
        seen_inputs.append(inputs)
        seen_mixed.append(mixed_rows)
        seen_upstream.append(upstream)
        input_grad = lax.map(lambda packed: section_back(*packed)[3], (w_proj, w_up, w_down, inputs, mixed_rows, upstream))
        if tick_index + 1 < TICKS:
            below_grad = input_grad[:, :, 0]
            skip_grad = input_grad[:, :, 1]
            from_above = jnp.concatenate([below_grad[1:], jnp.zeros_like(below_grad[:1])], axis=0)
            mirrored = skip_grad[::-1]
            upstream = (from_above.astype(jnp.float32) + encoder_weight * mirrored.astype(jnp.float32)).astype(jnp.bfloat16)
            upstream = upstream.at[SECTIONS - 1].set(loss_grads[tick_index])
    all_inputs = jnp.stack(seen_inputs, axis=1)
    all_mixed = jnp.stack(seen_mixed, axis=1)
    all_upstream = jnp.stack(seen_upstream, axis=1)

    def section_grads(packed):
        proj_weight, up_weight, down_weight, inputs_ticks, mixed_ticks, upstream_ticks = packed
        proj_total = jnp.zeros((REPLICAS, 2, D, D), jnp.float32)
        up_total = jnp.zeros((REPLICAS, D, FF), jnp.float32)
        down_total = jnp.zeros((REPLICAS, FF, D), jnp.float32)
        for tick_index in range(TICKS):
            inputs = inputs_ticks[tick_index]
            mixed_rows = mixed_ticks[tick_index]
            upstream_now = upstream_ticks[tick_index]
            activated, back_hidden, mixed_grad, unused_grad = section_back(proj_weight, up_weight, down_weight, inputs, mixed_rows, upstream_now)
            down_total = down_total + jnp.einsum('rmf,rmd->rfd', activated.reshape(REPLICAS, M, FF).astype(jnp.float32), upstream_now.reshape(REPLICAS, M, D).astype(jnp.float32))
            up_total = up_total + jnp.einsum('rmd,rmf->rdf', mixed_rows.reshape(REPLICAS, M, D).astype(jnp.float32), back_hidden.reshape(REPLICAS, M, FF).astype(jnp.float32))
            proj_total = proj_total + jnp.einsum('rmki,rmj->rkij', inputs.reshape(REPLICAS, M, 2, D).astype(jnp.float32), mixed_grad.reshape(REPLICAS, M, D).astype(jnp.float32))
        return finish(proj_total), finish(up_total), finish(down_total)

    grad_proj, grad_up, grad_down = lax.map(section_grads, (w_proj, w_up, w_down, all_inputs, all_mixed, all_upstream))
    return grad_proj, grad_up, grad_down, input_grad
```

```python
import jax
import jax.numpy as jnp
from jax import lax
from jax.sharding import PartitionSpec as P

gelu_scale = 0.7978845608
gelu_cubic = 0.044715
group = ("tensor", "replica")


def gelu_pair(pre_gelu):
    inner = gelu_scale * (pre_gelu + gelu_cubic * pre_gelu * pre_gelu * pre_gelu)
    tanh_part = jnp.tanh(inner)
    gelu_value = 0.5 * pre_gelu * (1.0 + tanh_part)
    gelu_slope = 0.5 * (1.0 + tanh_part) + 0.5 * pre_gelu * (
        1.0 - tanh_part * tanh_part
    ) * gelu_scale * (1.0 + 3.0 * gelu_cubic * pre_gelu * pre_gelu)
    return (gelu_value, gelu_slope)


def send_by(x, axes, size, by):
    return lax.ppermute(x, axes, [(i, (i + by) % size) for i in range(size)])


def gather_all(x, axes, size, me):
    parts = [x] + [send_by(x, axes, size, by) for by in range(1, size)]
    stacked = jnp.stack(parts)
    order = (me - jnp.arange(size)) % size
    return stacked[order]


def exchange(pieces, axes, size, me):
    own = lax.dynamic_index_in_dim(pieces, me, 0, keepdims=False)
    parts = [own]
    for by in range(1, size):
        piece = lax.dynamic_index_in_dim(pieces, (me + by) % size, 0, keepdims=False)
        parts.append(send_by(piece, axes, size, by))
    return parts


def body(pool_inputs, pool_mixed, crop_ids, incoming, loss_grads, w_proj, w_up, w_down):
    section_index = lax.axis_index("section")
    section_count = lax.axis_size("section")
    replicas = lax.axis_size("replica")
    tensors = lax.axis_size("tensor")
    members = replicas * tensors
    replica_index = lax.axis_index("replica")
    me = lax.axis_index("tensor") * replicas + replica_index
    bf16, f32 = jnp.bfloat16, jnp.float32
    proj, up, down = w_proj[0], w_up[0], w_down[0]
    own = proj.shape[1]
    rows = incoming.shape[1]
    width = up.shape[0]
    ticks = crop_ids.shape[1]
    encoder = section_index < section_count // 2
    encoder_weight = jnp.where(encoder, 1.0, 0.0).astype(f32)
    is_top = section_index == section_count - 1
    skip_mask = jnp.stack([jnp.ones((), bf16), jnp.where(encoder, 0.0, 1.0).astype(bf16)])

    ids = gather_all(crop_ids[0], "replica", replicas, replica_index)
    seed = gather_all(incoming[0], group, members, me)
    upstream = (
        seed.reshape(tensors, replicas, rows, -1).transpose(1, 2, 0, 3).reshape(replicas * rows, width)
    )
    mixed_pool = gather_all(pool_mixed[0], "replica", replicas, replica_index)
    order = (replica_index - jnp.arange(replicas)) % replicas

    def own_columns(x):
        cut = jnp.moveaxis(x.reshape(x.shape[:-1] + (replicas, own)), -2, 0)
        parts = exchange(cut, "replica", replicas, replica_index)
        return jnp.stack(parts)[order]

    inputs_pool = own_columns(pool_inputs[0]) * skip_mask[None, None, :, None]
    loss_own = jnp.moveaxis(own_columns(loss_grads), 0, 1).reshape(ticks - 1, replicas * rows, own)

    kept = []
    input_grad = None
    for tick_index in range(ticks):
        picked = ids[:, tick_index]
        inputs = jax.vmap(lambda pool, chosen: pool[chosen])(inputs_pool, picked)
        mixed = jax.vmap(lambda pool, chosen: pool[chosen])(mixed_pool, picked)
        mixed_rows = mixed.reshape(replicas * rows, width)
        value, slope = gelu_pair(jnp.dot(mixed_rows, up, preferred_element_type=f32))
        activated = value.astype(bf16)
        back_act = jnp.einsum("md,fd->mf", upstream, down, preferred_element_type=f32)
        back_hidden = (back_act * slope).astype(bf16)
        partial = jnp.einsum("mf,df->md", back_hidden, up, preferred_element_type=f32)
        pieces = partial.reshape(members, -1, width)
        parts = exchange(pieces.astype(bf16), group, members, me)
        total = lax.dynamic_index_in_dim(pieces, me, 0, keepdims=False)
        for part in parts[1:]:
            total = total + part.astype(f32)
        my_rows = lax.dynamic_index_in_dim(
            upstream.reshape(members, -1, width), me, 0, keepdims=False
        )
        my_grad = (my_rows.astype(f32) + total).astype(bf16)
        mixed_grad = gather_all(my_grad, group, members, me).reshape(replicas * rows, width)
        input_grad = jnp.einsum("mj,kij->kmi", mixed_grad, proj, preferred_element_type=f32).astype(bf16)
        kept.append((inputs, mixed, activated, back_hidden, mixed_grad, upstream))
        if tick_index + 1 < ticks:
            above = lax.ppermute(
                input_grad[0], "section", [(i, i - 1) for i in range(1, section_count)]
            )
            mirrored = lax.ppermute(
                input_grad[1],
                "section",
                [(i, section_count - 1 - i) for i in range(section_count // 2, section_count)],
            )
            summed = (above.astype(f32) + encoder_weight * mirrored.astype(f32)).astype(bf16)
            mine = jnp.where(is_top, loss_own[tick_index], summed)
            upstream = (
                gather_all(mine, group, members, me).transpose(1, 0, 2).reshape(replicas * rows, width)
            )

    def by_replica(index):
        return jnp.concatenate(
            [k[index].reshape((replicas, rows) + k[index].shape[(2 if index < 2 else 1):]) for k in kept],
            axis=1,
        )

    all_inputs, all_mixed, all_active, all_hidden, all_grads, all_upstream = (
        by_replica(i) for i in range(6)
    )

    def finish(spec, left, right):
        total = 0.0
        for r in range(replicas):
            one = jnp.einsum(spec, left[r], right[r], preferred_element_type=f32)
            total = total + one.astype(bf16).astype(f32)
        return total.astype(bf16)[None]

    grad_down = finish("mf,md->fd", all_active, all_upstream)
    grad_up = finish("md,mf->df", all_mixed, all_hidden)
    grad_proj = finish("mki,mj->kij", all_inputs, all_grads)
    cut = input_grad.reshape(2, replicas, rows, own).transpose(1, 2, 0, 3)
    parts = exchange(cut, "replica", replicas, replica_index)
    out = jnp.stack(parts)[order]
    outgoing = out.transpose(1, 2, 0, 3).reshape(rows, 2, replicas * own)
    return grad_proj, grad_up, grad_down, outgoing[None]


def solution(mesh):
    in_specs = (
        P("section", "replica", None, "tensor"),
        P("section", "replica", None),
        P("section", "replica", None),
        P("section", "replica", "tensor"),
        P(None, "replica", "tensor"),
        P("section", None, ("tensor", "replica"), None),
        P("section", None, ("tensor", "replica")),
        P("section", ("tensor", "replica"), None),
    )
    out_specs = (
        P("section", None, ("tensor", "replica"), None),
        P("section", None, ("tensor", "replica")),
        P("section", ("tensor", "replica"), None),
        P("section", "replica", None, "tensor"),
    )
    return jax.shard_map(body, mesh=mesh, in_specs=in_specs, out_specs=out_specs, check_vma=False)
```

```python
import functools

import jax
import jax.numpy as jnp
from jax import lax
from jax.experimental import pallas as pl
from jax.experimental.pallas import tpu as pltpu
from jax.sharding import PartitionSpec as P

gelu_scale = 0.7978845608
gelu_cubic = 0.044715
bf16, f32 = jnp.bfloat16, jnp.float32
MESH = pl.DeviceIdType.MESH


def gelu_pair(pre_gelu):
    inner = gelu_scale * (pre_gelu + gelu_cubic * pre_gelu * pre_gelu * pre_gelu)
    tanh_part = jnp.tanh(inner)
    gelu_value = 0.5 * pre_gelu * (1.0 + tanh_part)
    gelu_slope = 0.5 * (1.0 + tanh_part) + 0.5 * pre_gelu * (
        1.0 - tanh_part * tanh_part
    ) * gelu_scale * (1.0 + 3.0 * gelu_cubic * pre_gelu * pre_gelu)
    return (gelu_value, gelu_slope)


def dot(a, b):
    return jnp.dot(a, b, preferred_element_type=f32)


def dot_nt(a, b):
    return lax.dot_general(a, b, (((1,), (1,)), ((), ())), preferred_element_type=f32)


def ticks_kernel(
    sections, tensors, replicas, own, ticks,
    inputs_hbm, pool_hbm, ids_hbm, seed_hbm, loss_hbm, proj_hbm, up_hbm, down_hbm,
    inputs_t, pool, act_t, sum_hidden, sum_grad, sum_up, out_t,
    proj, up, down, in_src, pool_src, ids_src, seed_src, loss_src, ids, loss_t,
    upstream, grads, hidden, part, got, own_part, slope_hi, slope_lo, slope, edge, edge_got,
    acc_hidden, acc_grad, acc_up,
    load_sem, place_sem, pool_sems, inputs_sems, ids_sems, loss_sems, seed_sems,
    part_sems, grad_sems, up_sems, edge_sems, out_sems,
):
    members = tensors * replicas
    section = lax.axis_index("section")
    tensor = lax.axis_index("tensor")
    replica = lax.axis_index("replica")
    me = tensor * replicas + replica
    hidden_rows = down.shape[0]

    def device(s, member):
        return {
            "section": s,
            "tensor": lax.div(member, replicas),
            "replica": lax.rem(member, replicas),
        }

    def member_at(by):
        return lax.rem(me + by, members)

    def replica_at(by):
        return lax.rem(replica + by, replicas)

    def load(i, src, dst):
        copy = pltpu.make_async_copy(src, dst, load_sem.at[i])
        copy.start()
        return copy

    pairs = [
        (pool_hbm, pool_src), (seed_hbm, seed_src), (ids_hbm, ids_src), (inputs_hbm, in_src),
        (loss_hbm, loss_src), (up_hbm, up), (down_hbm, down), (proj_hbm, proj),
    ]
    loads = [load(i, src, dst) for i, (src, dst) in enumerate(pairs)]
    ld_pool, ld_seed, ld_ids, ld_in, ld_loss, ld_up, ld_down, ld_proj = loads

    barrier = pltpu.get_barrier_semaphore()
    above = lax.rem(section + 1, sections)
    below = lax.rem(section + sections - 1, sections)
    mirror = sections - 1 - section
    for by in range(1, members):
        pl.semaphore_signal(barrier, 1, device_id=device(section, member_at(by)), device_id_type=MESH)
    for other in (above, below, mirror):
        pl.semaphore_signal(barrier, 1, device_id=device(other, me), device_id_type=MESH)
    pl.semaphore_wait(barrier, members - 1 + 3)

    sent = []

    def send(src, dst, sems, index, target):
        copy = pltpu.make_async_remote_copy(
            src_ref=src, dst_ref=dst, send_sem=sems.at[(0,) + index], recv_sem=sems.at[(1,) + index],
            device_id=target, device_id_type=MESH,
        )
        copy.start()
        sent.append(copy)
        return copy

    def over_replicas(src_of, dst, sems):
        return [
            send(src_of(replica_at(by)), dst, sems, (by - 1,),
                 device(section, tensor * replicas + replica_at(by)))
            for by in range(1, replicas)
        ]

    def place(i, src, dst):
        copy = pltpu.make_async_copy(src, dst, place_sem.at[i])
        copy.start()
        return copy

    slab = pl.ds(pl.multiple_of(me * own, 16), own)
    wide = pl.ds(pl.multiple_of(tensor * (replicas * own), 16), replicas * own)
    ld_pool.wait()
    pool_in = over_replicas(lambda r: pool_src, pool.at[replica], pool_sems)
    places = [place(0, pool_src, pool.at[replica])]
    ld_seed.wait()
    seed_to = upstream.at[0, replica, wide]
    seed_in = [
        send(seed_src, seed_to, seed_sems, (by - 1,), device(section, member_at(by)))
        for by in range(1, members)
    ]
    places.append(place(1, seed_src, seed_to))
    ld_ids.wait()
    ids_in = over_replicas(lambda r: ids_src, ids.at[replica], ids_sems)
    places.append(place(2, ids_src, ids.at[replica]))
    ld_in.wait()
    inputs_in = over_replicas(lambda r: in_src.at[r], inputs_t.at[replica], inputs_sems)
    places.append(place(3, in_src.at[replica], inputs_t.at[replica]))
    ld_loss.wait()
    loss_in = over_replicas(lambda r: loss_src.at[r], loss_t.at[replica], loss_sems)
    places.append(place(4, loss_src.at[replica], loss_t.at[replica]))

    acc_hidden[...] = jnp.zeros_like(acc_hidden)
    acc_grad[...] = jnp.zeros_like(acc_grad)
    acc_up[...] = jnp.zeros_like(acc_up)

    ld_up.wait()
    places[0].wait()
    for copy in pool_in:
        copy.wait_recv()
    step = 128

    for r in range(replicas):
        def pre_step(c, carry, r=r):
            cols = pl.ds(pl.multiple_of(c * step, step), step)
            value, gelu_slope = gelu_pair(dot(pool[r], up[:, cols]).T)
            act_t[r, cols, :] = value.astype(bf16)
            high = gelu_slope.astype(bf16)
            slope_hi[r, cols, :] = high
            slope_lo[r, cols, :] = (gelu_slope - high.astype(f32)).astype(bf16)
            return carry
        lax.fori_loop(0, hidden_rows // step, pre_step, 0)

    places[2].wait()
    for copy in ids_in:
        copy.wait_recv()

    def picks(t, r):
        row = ids[r, pl.ds(t, 1), :]
        place_of = lax.broadcasted_iota(jnp.int32, (pool.shape[1], row.shape[1]), 0)
        return jnp.where(place_of == row, 1.0, 0.0).astype(bf16)

    def pick_slope(t, r):
        chosen = picks(t, r)
        slope[r] = dot(slope_hi[r], chosen) + dot(slope_lo[r], chosen)

    for r in range(replicas):
        pick_slope(0, r)

    ld_down.wait()
    ld_proj.wait()
    places[1].wait()
    for copy in seed_in:
        copy.wait_recv()

    up_in = {}
    part_in, grad_in, edge_in = {}, {}, {}

    def stage_hidden(t, r):
        for copy in up_in.get((t, r), ()):
            copy.wait_recv()
        hidden[t, r] = (dot(down[...], upstream[t, r]) * slope[r]).astype(bf16)
        copies = []
        for by in range(1, members):
            to = member_at(by)
            rows = pl.ds(pl.multiple_of(to * own, 16), own)
            part[t, r, by - 1] = dot(up[rows, :], hidden[t, r]).astype(bf16)
            copies.append(send(part.at[t, r, by - 1], got.at[t, r, by - 1], part_sems,
                               (t, r, by - 1), device(section, to)))
        own_part[r] = dot(up[slab, :], hidden[t, r]) + upstream[t, r, slab, :].astype(f32)
        part_in[t, r] = copies

    def stage_sum(t, r):
        total = own_part[r]
        for by in range(1, members):
            part_in[t, r][by - 1].wait_recv()
            total = total + got[t, r, by - 1].astype(f32)
        grads[t, r, slab, :] = total.astype(bf16)
        mine = grads.at[t, r, slab]
        grad_in[t, r] = [
            send(mine, mine, grad_sems, (t, r, by - 1), device(section, member_at(by)))
            for by in range(1, members)
        ]

    def stage_project(t, r):
        for copy in grad_in[t, r]:
            copy.wait_recv()
        edge[t, r, 1] = dot(proj[1], grads[t, r]).astype(bf16)
        last = t + 1 == ticks
        if not last:
            skip = pltpu.make_async_remote_copy(
                src_ref=edge.at[t, r, 1], dst_ref=edge_got.at[t, r, 1],
                send_sem=edge_sems.at[0, t, r, 1], recv_sem=edge_sems.at[1, t, r, 1],
                device_id=device(mirror, me), device_id_type=MESH,
            )
            pl.when(section >= sections // 2)(skip.start)
        edge[t, r, 0] = dot(proj[0], grads[t, r]).astype(bf16)
        if not last:
            down_copy = pltpu.make_async_remote_copy(
                src_ref=edge.at[t, r, 0], dst_ref=edge_got.at[t, r, 0],
                send_sem=edge_sems.at[0, t, r, 0], recv_sem=edge_sems.at[1, t, r, 0],
                device_id=device(below, me), device_id_type=MESH,
            )
            pl.when(section > 0)(down_copy.start)
            edge_in[t, r] = (down_copy, skip)

    def stage_next(t, r):
        down_copy, skip = edge_in[t, r]

        @pl.when(section < sections // 2)
        def _():
            down_copy.wait_recv()
            skip.wait_recv()
            summed = edge_got[t, r, 0].astype(f32) + edge_got[t, r, 1].astype(f32)
            upstream[t + 1, r, slab, :] = summed.astype(bf16)

        @pl.when((section >= sections // 2) & (section < sections - 1))
        def _():
            down_copy.wait_recv()
            upstream[t + 1, r, slab, :] = edge_got[t, r, 0]

        @pl.when(section == sections - 1)
        def _():
            upstream[t + 1, r, slab, :] = loss_t[r, t]

        mine = upstream.at[t + 1, r, slab]
        up_in[t + 1, r] = [
            send(mine, mine, up_sems, (t, r, by - 1), device(section, member_at(by)))
            for by in range(1, members)
        ]

    every = range(replicas)
    for t in range(ticks):
        for r in every:
            stage_hidden(t, r)
        for r in every:
            stage_sum(t, r)
        for r in every:
            chosen = picks(t, r)
            acc_hidden[r] += dot_nt(chosen, hidden[t, r])
            acc_up[r] += dot_nt(chosen, upstream[t, r])
        if t + 1 < ticks:
            for r in every:
                pick_slope(t + 1, r)
        if t == 0:
            places[3].wait()
            places[4].wait()
            for copy in inputs_in + loss_in:
                copy.wait_recv()
        for r in every:
            stage_project(t, r)
        for r in every:
            if t + 1 < ticks:
                stage_next(t, r)
        for r in every:
            acc_grad[r] += dot_nt(picks(t, r), grads[t, r])

    last = ticks - 1
    outs = []
    for by in range(1, replicas):
        to = replica_at(by)
        outs.append(send(edge.at[last, to], out_t.at[replica], out_sems, (by - 1,),
                         device(section, tensor * replicas + to)))
    out_place = place(5, edge.at[last, replica], out_t.at[replica])
    sum_hidden[...] = acc_hidden[...].astype(bf16)
    sum_grad[...] = acc_grad[...].astype(bf16)
    sum_up[...] = acc_up[...].astype(bf16)
    for copy in outs:
        copy.wait_recv()
    out_place.wait()
    for copy in sent:
        copy.wait_send()
    for key in edge_in:
        down_copy, skip = edge_in[key]
        pl.when(section > 0)(down_copy.wait_send)
        pl.when(section >= sections // 2)(skip.wait_send)


def body(pool_inputs, pool_mixed, crop_ids, incoming, loss_grads, w_proj, w_up, w_down):
    sections = lax.axis_size("section")
    tensors, replicas = lax.axis_size("tensor"), lax.axis_size("replica")
    members = tensors * replicas
    encoder = lax.axis_index("section") < sections // 2
    own = w_proj.shape[2]
    own_p = -(-own // 16) * 16
    rows, width = incoming.shape[1], w_up.shape[1]
    width_p = members * own_p
    hidden = w_up.shape[2]
    ticks = crop_ids.shape[1]
    saved = pool_mixed.shape[1]

    def padded(x, axis):
        if own == own_p:
            return x
        count = x.shape[axis] // own
        shape = x.shape[:axis] + (count, own) + x.shape[axis + 1:]
        fill = [(0, 0)] * (x.ndim + 1)
        fill[axis + 1] = (0, own_p - own)
        shape_p = x.shape[:axis] + (count * own_p,) + x.shape[axis + 1:]
        return jnp.pad(x.reshape(shape), fill).reshape(shape_p)

    proj = padded(padded(w_proj[0], 1), 2)
    up, down = padded(w_up[0], 0), padded(w_down[0], 1)
    pool_own = padded(pool_mixed[0], 1)
    mask = jnp.stack([jnp.ones((), bf16), jnp.where(encoder, 0.0, 1.0).astype(bf16)])
    features = (pool_inputs[0] * mask[None, :, None]).transpose(1, 2, 0)
    features = features.reshape(2, replicas, own, saved).transpose(1, 0, 2, 3)
    features = padded(features, 2)
    seed = padded(incoming[0].T, 0)
    loss = loss_grads.transpose(0, 2, 1).reshape(ticks - 1, replicas, own, rows)
    loss = padded(loss.transpose(1, 0, 2, 3), 2)

    shape = jax.ShapeDtypeStruct
    vmem = pl.BlockSpec(memory_space=pltpu.VMEM)
    hbm = pl.BlockSpec(memory_space=pl.ANY)
    dma = pltpu.SemaphoreType.DMA
    scratch = [
        pltpu.VMEM(proj.shape, bf16), pltpu.VMEM(up.shape, bf16), pltpu.VMEM(down.shape, bf16),
        pltpu.VMEM(features.shape, bf16), pltpu.VMEM(pool_own.shape, bf16),
        pltpu.VMEM(crop_ids.shape[1:], jnp.int32), pltpu.VMEM(seed.shape, bf16),
        pltpu.VMEM(loss.shape, bf16), pltpu.VMEM((replicas,) + crop_ids.shape[1:], jnp.int32),
        pltpu.VMEM((replicas, ticks - 1, own_p, rows), bf16),
        pltpu.VMEM((ticks, replicas, width_p, rows), bf16),
        pltpu.VMEM((ticks, replicas, width_p, rows), bf16),
        pltpu.VMEM((ticks, replicas, hidden, rows), bf16),
        pltpu.VMEM((ticks, replicas, members - 1, own_p, rows), bf16),
        pltpu.VMEM((ticks, replicas, members - 1, own_p, rows), bf16),
        pltpu.VMEM((replicas, own_p, rows), f32),
        pltpu.VMEM((replicas, hidden, saved), bf16), pltpu.VMEM((replicas, hidden, saved), bf16),
        pltpu.VMEM((replicas, hidden, rows), f32),
        pltpu.VMEM((ticks, replicas, 2, own_p, rows), bf16),
        pltpu.VMEM((ticks - 1, replicas, 2, own_p, rows), bf16),
        pltpu.VMEM((replicas, saved, hidden), f32), pltpu.VMEM((replicas, saved, width_p), f32),
        pltpu.VMEM((replicas, saved, width_p), f32),
        dma((8,)), dma((6,)), dma((2, replicas - 1)), dma((2, replicas - 1)), dma((2, replicas - 1)),
        dma((2, replicas - 1)), dma((2, members - 1)),
        dma((2, ticks, replicas, members - 1)), dma((2, ticks, replicas, members - 1)),
        dma((2, ticks - 1, replicas, members - 1)), dma((2, ticks - 1, replicas, 2)),
        dma((2, replicas - 1)),
    ]
    inputs_t, pool, act_t, sum_hidden, sum_grad, sum_up, out_t = pl.pallas_call(
        functools.partial(ticks_kernel, sections, tensors, replicas, own_p, ticks),
        out_shape=(
            shape((replicas, 2, own_p, saved), bf16),
            shape((replicas, saved, width_p), bf16),
            shape((replicas, hidden, saved), bf16),
            shape((replicas, saved, hidden), bf16),
            shape((replicas, saved, width_p), bf16),
            shape((replicas, saved, width_p), bf16),
            shape((replicas, 2, own_p, rows), bf16),
        ),
        in_specs=[hbm] * 8,
        out_specs=(vmem,) * 7,
        scratch_shapes=scratch,
        compiler_params=pltpu.CompilerParams(
            collective_id=0, has_side_effects=True, vmem_limit_bytes=60 * 1024 * 1024
        ),
        name="ticks",
    )(features, pool_own, crop_ids[0], seed, loss, proj, up, down)

    def trimmed(x, axis):
        if own == own_p:
            return x
        count = x.shape[axis] // own_p
        x = x.reshape(x.shape[:axis] + (count, own_p) + x.shape[axis + 1:])
        x = lax.slice_in_dim(x, 0, own, axis=axis + 1)
        return x.reshape(x.shape[:axis] + (count * own,) + x.shape[axis + 2:])

    def finish(spec, left, right):
        total = 0.0
        for r in range(replicas):
            one = jnp.einsum(spec, left[r], right[r], preferred_element_type=f32)
            total = total + one.astype(bf16).astype(f32)
        return total.astype(bf16)

    grad_down = trimmed(finish("fp,pd->fd", act_t, sum_up), 1)[None]
    grad_up = trimmed(finish("pd,pf->df", pool, sum_hidden), 0)[None]
    grad_proj = trimmed(trimmed(finish("kip,pj->kij", inputs_t, sum_grad), 1), 2)[None]
    outgoing = trimmed(out_t, 2).transpose(3, 1, 0, 2).reshape(rows, 2, replicas * own)
    return grad_proj, grad_up, grad_down, outgoing[None]


def solution(mesh):
    in_specs = (
        P("section", "replica", None, "tensor"),
        P("section", "replica", None),
        P("section", "replica", None),
        P("section", "replica", "tensor"),
        P(None, "replica", "tensor"),
        P("section", None, ("tensor", "replica"), None),
        P("section", None, ("tensor", "replica")),
        P("section", ("tensor", "replica"), None),
    )
    out_specs = (
        P("section", None, ("tensor", "replica"), None),
        P("section", None, ("tensor", "replica")),
        P("section", ("tensor", "replica"), None),
        P("section", "replica", None, "tensor"),
    )
    return jax.shard_map(body, mesh=mesh, in_specs=in_specs, out_specs=out_specs, check_vma=False)
```

```python
import functools

import jax
import jax.numpy as jnp
from jax import lax
from jax.experimental import pallas as pl
from jax.experimental.pallas import tpu as pltpu
from jax.sharding import PartitionSpec as P

gelu_scale = 0.7978845608
gelu_cubic = 0.044715
bf16, f32 = jnp.bfloat16, jnp.float32
MESH = pl.DeviceIdType.MESH


def gelu_pair(pre_gelu):
    inner = gelu_scale * (pre_gelu + gelu_cubic * pre_gelu * pre_gelu * pre_gelu)
    tanh_part = jnp.tanh(inner)
    gelu_value = 0.5 * pre_gelu * (1.0 + tanh_part)
    gelu_slope = 0.5 * (1.0 + tanh_part) + 0.5 * pre_gelu * (
        1.0 - tanh_part * tanh_part
    ) * gelu_scale * (1.0 + 3.0 * gelu_cubic * pre_gelu * pre_gelu)
    return (gelu_value, gelu_slope)


def dot(a, b):
    return jnp.dot(a, b, preferred_element_type=f32)


def dot_nt(a, b):
    return lax.dot_general(a, b, (((1,), (1,)), ((), ())), preferred_element_type=f32)


def ticks_kernel(
    sections, tensors, replicas, own, ticks,
    inputs_hbm, pool_hbm, ids_hbm, seed_hbm, loss_hbm, proj_hbm, up_hbm, down_hbm,
    inputs_t, pool, act_t, sum_hidden, sum_grad, sum_up, out_t,
    proj, up, down, in_src, pool_src, ids_src, seed_src, loss_src, ids, loss_t,
    upstream, grads, hidden, part, got, own_part, slope_hi, slope_lo, slope, edge, edge_got,
    acc_hidden, acc_grad, acc_up,
    load_sem, place_sem, pool_sems, inputs_sems, ids_sems, loss_sems, seed_sems,
    part_sems, grad_sems, up_sems, edge_sems, out_sems,
):
    members = tensors * replicas
    section = lax.axis_index("section")
    tensor = lax.axis_index("tensor")
    replica = lax.axis_index("replica")
    me = tensor * replicas + replica
    hidden_rows = down.shape[0]

    def device(s, member):
        return {
            "section": s,
            "tensor": lax.div(member, replicas),
            "replica": lax.rem(member, replicas),
        }

    def member_at(by):
        return lax.rem(me + by, members)

    def replica_at(by):
        return lax.rem(replica + by, replicas)

    def load(i, src, dst):
        copy = pltpu.make_async_copy(src, dst, load_sem.at[i])
        copy.start()
        return copy

    pairs = [
        (pool_hbm, pool_src), (seed_hbm, seed_src), (ids_hbm, ids_src), (inputs_hbm, in_src),
        (loss_hbm, loss_src), (up_hbm, up), (down_hbm, down), (proj_hbm, proj),
    ]
    loads = [load(i, src, dst) for i, (src, dst) in enumerate(pairs)]
    ld_pool, ld_seed, ld_ids, ld_in, ld_loss, ld_up, ld_down, ld_proj = loads

    barrier = pltpu.get_barrier_semaphore()
    above = lax.rem(section + 1, sections)
    below = lax.rem(section + sections - 1, sections)
    mirror = sections - 1 - section
    for by in range(1, members):
        pl.semaphore_signal(barrier, 1, device_id=device(section, member_at(by)), device_id_type=MESH)
    for other in (above, below, mirror):
        pl.semaphore_signal(barrier, 1, device_id=device(other, me), device_id_type=MESH)
    pl.semaphore_wait(barrier, members - 1 + 3)

    sent = []

    def send(src, dst, sems, index, target):
        copy = pltpu.make_async_remote_copy(
            src_ref=src, dst_ref=dst, send_sem=sems.at[(0,) + index], recv_sem=sems.at[(1,) + index],
            device_id=target, device_id_type=MESH,
        )
        copy.start()
        sent.append(copy)
        return copy

    def over_replicas(src_of, dst, sems):
        return [
            send(src_of(replica_at(by)), dst, sems, (by - 1,),
                 device(section, tensor * replicas + replica_at(by)))
            for by in range(1, replicas)
        ]

    def place(i, src, dst):
        copy = pltpu.make_async_copy(src, dst, place_sem.at[i])
        copy.start()
        return copy

    slab = pl.ds(pl.multiple_of(me * own, 16), own)
    wide = pl.ds(pl.multiple_of(tensor * (replicas * own), 16), replicas * own)
    ld_pool.wait()
    pool_in = over_replicas(lambda r: pool_src, pool.at[replica], pool_sems)
    places = [place(0, pool_src, pool.at[replica])]
    ld_ids.wait()
    ids_in = over_replicas(lambda r: ids_src, ids.at[replica], ids_sems)
    ld_seed.wait()
    seed_to = upstream.at[0, replica, wide]
    seed_in = [
        send(seed_src, seed_to, seed_sems, (by - 1,), device(section, member_at(by)))
        for by in range(1, members)
    ]
    places.append(place(1, seed_src, seed_to))
    places.append(place(2, ids_src, ids.at[replica]))
    ld_in.wait()
    places.append(place(3, in_src.at[replica], inputs_t.at[replica]))
    ld_loss.wait()
    places.append(place(4, loss_src.at[replica], loss_t.at[replica]))
    is_top = section == sections - 1
    loss_in = []
    for by in range(1, replicas):
        to = replica_at(by)
        loss_in.append(pltpu.make_async_remote_copy(
            src_ref=loss_src.at[to], dst_ref=loss_t.at[replica],
            send_sem=loss_sems.at[0, by - 1], recv_sem=loss_sems.at[1, by - 1],
            device_id=device(section, tensor * replicas + to), device_id_type=MESH,
        ))

    acc_hidden[...] = jnp.zeros_like(acc_hidden)
    acc_grad[...] = jnp.zeros_like(acc_grad)
    acc_up[...] = jnp.zeros_like(acc_up)

    ld_up.wait()
    places[0].wait()
    step = 128

    for by in range(replicas):
        r = lax.rem(replica + replicas - by, replicas)
        if by > 0:
            pool_in[by - 1].wait_recv()

        def pre_at(cols, r=r):
            value, gelu_slope = gelu_pair(dot(pool[r], up[:, cols]).T)
            act_t[r, cols, :] = value.astype(bf16)
            high = gelu_slope.astype(bf16)
            slope_hi[r, cols, :] = high
            slope_lo[r, cols, :] = (gelu_slope - high.astype(f32)).astype(bf16)

        @pl.loop(0, hidden_rows // step)
        def _(c):
            pre_at(pl.ds(pl.multiple_of(c * step, step), step))

        if hidden_rows % step:
            pre_at(pl.ds(hidden_rows - hidden_rows % step, hidden_rows % step))

    places[2].wait()
    for copy in ids_in:
        copy.wait_recv()

    def picks(t, r):
        row = ids[r, pl.ds(t, 1), :]
        place_of = lax.broadcasted_iota(jnp.int32, (pool.shape[1], row.shape[1]), 0)
        return jnp.where(place_of == row, 1.0, 0.0).astype(bf16)

    def pick_slope(t, r):
        chosen = picks(t, r)
        slope[r] = dot(slope_hi[r], chosen) + dot(slope_lo[r], chosen)

    for r in range(replicas):
        pick_slope(0, r)

    ld_down.wait()
    ld_proj.wait()
    places[1].wait()
    for copy in seed_in:
        copy.wait_recv()

    up_in = {}
    part_in, grad_in, edge_in = {}, {}, {}

    def stage_hidden(t, r):
        for copy in up_in.get((t, r), ()):
            copy.wait_recv()
        hidden[t, r] = (dot(down[...], upstream[t, r]) * slope[r]).astype(bf16)
        copies = []
        for by in range(1, members):
            to = member_at(by)
            rows = pl.ds(pl.multiple_of(to * own, 16), own)
            part[t, r, by - 1] = dot(up[rows, :], hidden[t, r]).astype(bf16)
            copies.append(send(part.at[t, r, by - 1], got.at[t, r, by - 1], part_sems,
                               (t, r, by - 1), device(section, to)))
        own_part[r] = dot(up[slab, :], hidden[t, r]) + upstream[t, r, slab, :].astype(f32)
        part_in[t, r] = copies

    def stage_sum(t, r):
        total = own_part[r]
        for by in range(1, members):
            part_in[t, r][by - 1].wait_recv()
            total = total + got[t, r, by - 1].astype(f32)
        grads[t, r, slab, :] = total.astype(bf16)
        mine = grads.at[t, r, slab]
        grad_in[t, r] = [
            send(mine, mine, grad_sems, (t, r, by - 1), device(section, member_at(by)))
            for by in range(1, members)
        ]

    def stage_project(t, r):
        for copy in grad_in[t, r]:
            copy.wait_recv()
        edge[t, r, 1] = dot(proj[1], grads[t, r]).astype(bf16)
        last = t + 1 == ticks
        if not last:
            skip = pltpu.make_async_remote_copy(
                src_ref=edge.at[t, r, 1], dst_ref=edge_got.at[t, r, 1],
                send_sem=edge_sems.at[0, t, r, 1], recv_sem=edge_sems.at[1, t, r, 1],
                device_id=device(mirror, me), device_id_type=MESH,
            )
            pl.when(section >= sections // 2)(skip.start)
        edge[t, r, 0] = dot(proj[0], grads[t, r]).astype(bf16)
        if not last:
            down_copy = pltpu.make_async_remote_copy(
                src_ref=edge.at[t, r, 0], dst_ref=edge_got.at[t, r, 0],
                send_sem=edge_sems.at[0, t, r, 0], recv_sem=edge_sems.at[1, t, r, 0],
                device_id=device(below, me), device_id_type=MESH,
            )
            pl.when(section > 0)(down_copy.start)
            edge_in[t, r] = (down_copy, skip)

    def stage_next(t, r):
        down_copy, skip = edge_in[t, r]

        @pl.when(section < sections // 2)
        def _():
            down_copy.wait_recv()
            skip.wait_recv()
            summed = edge_got[t, r, 0].astype(f32) + edge_got[t, r, 1].astype(f32)
            upstream[t + 1, r, slab, :] = summed.astype(bf16)

        @pl.when((section >= sections // 2) & (section < sections - 1))
        def _():
            down_copy.wait_recv()
            upstream[t + 1, r, slab, :] = edge_got[t, r, 0]

        @pl.when(section == sections - 1)
        def _():
            upstream[t + 1, r, slab, :] = loss_t[r, t]

        mine = upstream.at[t + 1, r, slab]
        up_in[t + 1, r] = [
            send(mine, mine, up_sems, (t, r, by - 1), device(section, member_at(by)))
            for by in range(1, members)
        ]

    every = range(replicas)
    for t in range(ticks):
        for r in every:
            stage_hidden(t, r)
        if t == 0:
            for copy in loss_in:
                pl.when(is_top)(copy.start)
        for r in every:
            stage_sum(t, r)
        for r in every:
            chosen = picks(t, r)
            acc_hidden[r] += dot_nt(chosen, hidden[t, r])
            acc_up[r] += dot_nt(chosen, upstream[t, r])
        if t + 1 < ticks:
            for r in every:
                pick_slope(t + 1, r)
        if t == 0:
            places[4].wait()
            for copy in loss_in:
                pl.when(is_top)(copy.wait_recv)
        for r in every:
            stage_project(t, r)
        if t == min(1, ticks - 1):
            inputs_in = over_replicas(lambda r: in_src.at[r], inputs_t.at[replica], inputs_sems)
        for r in every:
            if t + 1 < ticks:
                stage_next(t, r)
        for r in every:
            acc_grad[r] += dot_nt(picks(t, r), grads[t, r])

    last = ticks - 1
    outs = []
    for by in range(1, replicas):
        to = replica_at(by)
        outs.append(send(edge.at[last, to], out_t.at[replica], out_sems, (by - 1,),
                         device(section, tensor * replicas + to)))
    out_place = place(5, edge.at[last, replica], out_t.at[replica])
    sum_hidden[...] = acc_hidden[...].astype(bf16)
    sum_grad[...] = acc_grad[...].astype(bf16)
    sum_up[...] = acc_up[...].astype(bf16)
    for copy in outs + inputs_in:
        copy.wait_recv()
    out_place.wait()
    places[3].wait()
    for copy in loss_in:
        pl.when(is_top)(copy.wait_send)
    for copy in sent:
        copy.wait_send()
    for key in edge_in:
        down_copy, skip = edge_in[key]
        pl.when(section > 0)(down_copy.wait_send)
        pl.when(section >= sections // 2)(skip.wait_send)


def tail_kernel(
    replicas, keep_ref, act_t, pool, inputs_t, sum_hidden, sum_grad, sum_up,
    down_out, up_out, proj_out, down_v, up_v, proj_v, sems,
):
    copies = []

    def finish(term, rows, kept, out, scale=None):
        total = 0.0
        for r in range(replicas):
            total = total + term(r).astype(bf16).astype(f32)
        if scale is not None:
            total = total * scale
        kept.at[rows][...] = total.astype(bf16)
        copy = pltpu.make_async_copy(kept.at[rows], out.at[rows], sems.at[len(copies)])
        copy.start()
        copies.append(copy)

    for start in range(0, down_v.shape[0], 128):
        rows = pl.ds(start, min(128, down_v.shape[0] - start))
        finish(lambda r: dot(act_t[r, rows, :], sum_up[r]), rows, down_v, down_out)
    half = proj_v.shape[1] // 2
    for k in range(2):
        for start in (0, half):
            rows = (k, pl.ds(start, half))
            finish(lambda r: dot(inputs_t[r, k, pl.ds(start, half), :], sum_grad[r]), rows,
                   proj_v, proj_out, keep_ref[0] if k else None)
    for start in range(0, up_v.shape[0], 128):
        rows = pl.ds(start, min(128, up_v.shape[0] - start))
        finish(lambda r: dot(pool[r, :, rows].T, sum_hidden[r]), rows, up_v, up_out)
    for copy in copies:
        copy.wait()


def body(pool_inputs, pool_mixed, crop_ids, incoming, loss_grads, w_proj, w_up, w_down):
    sections = lax.axis_size("section")
    tensors, replicas = lax.axis_size("tensor"), lax.axis_size("replica")
    members = tensors * replicas
    encoder = lax.axis_index("section") < sections // 2
    own = w_proj.shape[2]
    own_p = -(-own // 16) * 16
    rows, width = incoming.shape[1], w_up.shape[1]
    width_p = members * own_p
    hidden = w_up.shape[2]
    ticks = crop_ids.shape[1]
    saved = pool_mixed.shape[1]

    def padded(x, axis):
        if own == own_p:
            return x
        count = x.shape[axis] // own
        shape = x.shape[:axis] + (count, own) + x.shape[axis + 1:]
        fill = [(0, 0)] * (x.ndim + 1)
        fill[axis + 1] = (0, own_p - own)
        shape_p = x.shape[:axis] + (count * own_p,) + x.shape[axis + 1:]
        return jnp.pad(x.reshape(shape), fill).reshape(shape_p)

    proj = padded(padded(w_proj[0], 1), 2)
    up, down = padded(w_up[0], 0), padded(w_down[0], 1)
    pool_own = padded(pool_mixed[0], 1)
    keep = jnp.where(encoder, 0.0, 1.0).astype(f32)[None]
    features = pool_inputs[0].transpose(1, 2, 0)
    features = features.reshape(2, replicas, own, saved).transpose(1, 0, 2, 3)
    features = padded(features, 2)
    seed = padded(incoming[0].T, 0)
    loss = loss_grads.transpose(0, 2, 1).reshape(ticks - 1, replicas, own, rows)
    loss = padded(loss.transpose(1, 0, 2, 3), 2)

    shape = jax.ShapeDtypeStruct
    vmem = pl.BlockSpec(memory_space=pltpu.VMEM)
    hbm = pl.BlockSpec(memory_space=pl.ANY)
    dma = pltpu.SemaphoreType.DMA
    scratch = [
        pltpu.VMEM(proj.shape, bf16), pltpu.VMEM(up.shape, bf16), pltpu.VMEM(down.shape, bf16),
        pltpu.VMEM(features.shape, bf16), pltpu.VMEM(pool_own.shape, bf16),
        pltpu.VMEM(crop_ids.shape[1:], jnp.int32), pltpu.VMEM(seed.shape, bf16),
        pltpu.VMEM(loss.shape, bf16), pltpu.VMEM((replicas,) + crop_ids.shape[1:], jnp.int32),
        pltpu.VMEM((replicas, ticks - 1, own_p, rows), bf16),
        pltpu.VMEM((ticks, replicas, width_p, rows), bf16),
        pltpu.VMEM((ticks, replicas, width_p, rows), bf16),
        pltpu.VMEM((ticks, replicas, hidden, rows), bf16),
        pltpu.VMEM((ticks, replicas, members - 1, own_p, rows), bf16),
        pltpu.VMEM((ticks, replicas, members - 1, own_p, rows), bf16),
        pltpu.VMEM((replicas, own_p, rows), f32),
        pltpu.VMEM((replicas, hidden, saved), bf16), pltpu.VMEM((replicas, hidden, saved), bf16),
        pltpu.VMEM((replicas, hidden, rows), f32),
        pltpu.VMEM((ticks, replicas, 2, own_p, rows), bf16),
        pltpu.VMEM((ticks - 1, replicas, 2, own_p, rows), bf16),
        pltpu.VMEM((replicas, saved, hidden), f32), pltpu.VMEM((replicas, saved, width_p), f32),
        pltpu.VMEM((replicas, saved, width_p), f32),
        dma((8,)), dma((6,)), dma((2, replicas - 1)), dma((2, replicas - 1)), dma((2, replicas - 1)),
        dma((2, replicas - 1)), dma((2, members - 1)),
        dma((2, ticks, replicas, members - 1)), dma((2, ticks, replicas, members - 1)),
        dma((2, ticks - 1, replicas, members - 1)), dma((2, ticks - 1, replicas, 2)),
        dma((2, replicas - 1)),
    ]
    inputs_t, pool, act_t, sum_hidden, sum_grad, sum_up, out_t = pl.pallas_call(
        functools.partial(ticks_kernel, sections, tensors, replicas, own_p, ticks),
        out_shape=(
            shape((replicas, 2, own_p, saved), bf16),
            shape((replicas, saved, width_p), bf16),
            shape((replicas, hidden, saved), bf16),
            shape((replicas, saved, hidden), bf16),
            shape((replicas, saved, width_p), bf16),
            shape((replicas, saved, width_p), bf16),
            shape((replicas, 2, own_p, rows), bf16),
        ),
        in_specs=[hbm] * 8,
        out_specs=(vmem,) * 7,
        scratch_shapes=scratch,
        compiler_params=pltpu.CompilerParams(
            collective_id=0, has_side_effects=True, vmem_limit_bytes=60 * 1024 * 1024
        ),
        name="ticks",
    )(features, pool_own, crop_ids[0], seed, loss, proj, up, down)

    def trimmed(x, axis):
        if own == own_p:
            return x
        count = x.shape[axis] // own_p
        x = x.reshape(x.shape[:axis] + (count, own_p) + x.shape[axis + 1:])
        x = lax.slice_in_dim(x, 0, own, axis=axis + 1)
        return x.reshape(x.shape[:axis] + (count * own,) + x.shape[axis + 2:])

    grad_down, grad_up, grad_proj = pl.pallas_call(
        functools.partial(tail_kernel, replicas),
        out_shape=(
            shape((hidden, width_p), bf16), shape((width_p, hidden), bf16),
            shape((2, own_p, width_p), bf16),
        ),
        in_specs=[pl.BlockSpec(memory_space=pltpu.SMEM)] + [vmem] * 6,
        out_specs=(hbm,) * 3,
        scratch_shapes=[
            pltpu.VMEM((hidden, width_p), bf16), pltpu.VMEM((width_p, hidden), bf16),
            pltpu.VMEM((2, own_p, width_p), bf16),
            dma((-(-hidden // 128) - (-width_p // 128) + 4,)),
        ],
        compiler_params=pltpu.CompilerParams(vmem_limit_bytes=40 * 1024 * 1024),
        name="tail",
    )(keep, act_t, pool, inputs_t, sum_hidden, sum_grad, sum_up)
    grad_down = trimmed(grad_down, 1)[None]
    grad_up = trimmed(grad_up, 0)[None]
    grad_proj = trimmed(trimmed(grad_proj, 1), 2)[None]
    outgoing = trimmed(out_t, 2).transpose(3, 1, 0, 2).reshape(rows, 2, replicas * own)
    return grad_proj, grad_up, grad_down, outgoing[None]


def solution(mesh):
    in_specs = (
        P("section", "replica", None, "tensor"),
        P("section", "replica", None),
        P("section", "replica", None),
        P("section", "replica", "tensor"),
        P(None, "replica", "tensor"),
        P("section", None, ("tensor", "replica"), None),
        P("section", None, ("tensor", "replica")),
        P("section", ("tensor", "replica"), None),
    )
    out_specs = (
        P("section", None, ("tensor", "replica"), None),
        P("section", None, ("tensor", "replica")),
        P("section", ("tensor", "replica"), None),
        P("section", "replica", None, "tensor"),
    )
    return jax.shard_map(body, mesh=mesh, in_specs=in_specs, out_specs=out_specs, check_vma=False)
```
